32 devices in a mesh: seq: 4 (over z), ctx: 8 (over y, x, core).
Axes of the slice: x: 2, y: 2, z: 4, core: 2. Of those that a mesh axis runs over, the one named last changes fastest.
Arguments:
- layer_input: bfloat16 [12, 1024, 768], P('seq', 'ctx'), may hold values from -6 to 6
- doc_lengths: int32 [12, 4], P('seq'), may hold values from 1 to 512, 1024 in all within a row
- query_weight: bfloat16 [768, 768], P(('seq', 'ctx')), may hold values from -0.3125 to 0.3125
- key_weight: bfloat16 [768, 768], P(('seq', 'ctx')), may hold values from -0.3125 to 0.3125
- value_weight: bfloat16 [768, 768], P(('seq', 'ctx')), may hold values from -0.21875 to 0.21875
- output_weight: bfloat16 [768, 768], P(('seq', 'ctx')), may hold values from -0.875 to 0.875
- query_bias: bfloat16 [768], P(('seq', 'ctx')), may hold values from -3 to 3
- value_bias: bfloat16 [768], P(('seq', 'ctx')), may hold values from -3 to 3
- output_bias: bfloat16 [768], P(('seq', 'ctx')), may hold values from -3 to 3
- first_gain: bfloat16 [768], P(('seq', 'ctx')), may hold values from 0.5 to 1.5
- first_shift: bfloat16 [768], P(('seq', 'ctx')), may hold values from -2 to 2
- inner_weight: bfloat16 [768, 3072], P(('seq', 'ctx')), may hold values from -0.21875 to 0.21875
- inner_bias: bfloat16 [3072], P(('seq', 'ctx')), may hold values from -3 to 3
- outer_weight: bfloat16 [3072, 768], P(('seq', 'ctx')), may hold values from -0.109375 to 0.109375
- outer_bias: bfloat16 [768], P(('seq', 'ctx')), may hold values from -3 to 3
- second_gain: bfloat16 [768], P(('seq', 'ctx')), may hold values from 0.5 to 1.5
- second_shift: bfloat16 [768], P(('seq', 'ctx')), may hold values from -2 to 2
- output_cotangent: bfloat16 [12, 1024, 768], P('seq', 'ctx'), may hold values from -6 to 6
Outputs:
- layer_output: bfloat16 [12, 1024, 768], P('seq', 'ctx')
- input_grad: bfloat16 [12, 1024, 768], P('seq', 'ctx')
- query_weight_grad: float32 [768, 768], P(('seq', 'ctx'))
- key_weight_grad: float32 [768, 768], P(('seq', 'ctx'))
- value_weight_grad: float32 [768, 768], P(('seq', 'ctx'))
- output_weight_grad: float32 [768, 768], P(('seq', 'ctx'))
- query_bias_grad: float32 [768], P(('seq', 'ctx'))
- value_bias_grad: float32 [768], P(('seq', 'ctx'))
- output_bias_grad: float32 [768], P(('seq', 'ctx'))
- first_gain_grad: float32 [768], P(('seq', 'ctx'))
- first_shift_grad: float32 [768], P(('seq', 'ctx'))
- inner_weight_grad: float32 [768, 3072], P(('seq', 'ctx'))
- inner_bias_grad: float32 [3072], P(('seq', 'ctx'))
- outer_weight_grad: float32 [3072, 768], P(('seq', 'ctx'))
- outer_bias_grad: float32 [768], P(('seq', 'ctx'))
- second_gain_grad: float32 [768], P(('seq', 'ctx'))
- second_shift_grad: float32 [768], P(('seq', 'ctx'))
The draws below stay inside these ranges and needn't reach their ends.
Inputs may be any that keep to these rules, and one draw needn't show every extreme that they name: `doc_lengths`: each row holds the lengths of the 4 documents of one sequence in order; they sum to 1024, and the longest is exactly 512.
All inputs are finite; a program needn't handle non-finite values.
Results may differ from the reference program's by a relative error of at most 0.015.
Values may be sent and summed in bfloat16 or wider, within the bound.
A program may use at most 448 MiB of HBM per device.

```python
import math
import jax
import jax.numpy as jnp
import numpy as np
from jax import lax

D = 768
FF = 3072
HEADS = 12
HEAD_DIM = 64
SEQ_LEN = 1024
SEQUENCES = 12
DOCS = 4
DOC_MOST = 512


def draw_layer_input(key, part):
    shape = (SEQUENCES, SEQ_LEN, D)
    values = jnp.clip(jax.random.normal(key, shape, jnp.float32), -6.0, 6.0)
    return values.astype(jnp.bfloat16)


def level_of(own_key, extent, split, low, high):
    level = 1.0
    for dim, parts in split:
        steps = jax.random.uniform(jax.random.fold_in(jax.random.fold_in(own_key, 6), dim), (parts,), jnp.float32, low / len(split), high / len(split))
        level = level * jnp.repeat(jnp.exp(steps), extent[dim] // parts).reshape((-1,) + (1,) * (len(extent) - 1 - dim))
    return level


def length_profile(count, total, most, slope):
    portions = [(1 << 20) // math.isqrt(grade ** slope) + 1 for grade in range(2, count + 1)]
    rest, holding = total - most - (count - 1), [1] * (count - 1)
    while rest > 0:
        candidates = [i for i in range(count - 1) if holding[i] < most]
        mass, left = sum([portions[i] for i in candidates]), rest
        for i in candidates:
            more = min(most - holding[i], max(1, left * portions[i] // mass), rest)
            holding[i] = holding[i] + more
            rest = rest - more
    return np.array([most] + holding)


def uneven(own_key, count, total, reach, slope):
    if count == 2:
        one = jax.random.randint(own_key, (), max(1, total - reach), min(reach, total - 1) + 1)
        return jnp.stack([one, total - one])
    sizes = jnp.asarray(length_profile(count, total, reach, slope), jnp.int32)
    twos = (count - 1) // 2
    source_of, receiver = sizes[1:1 + 2 * twos:2], sizes[2:2 + 2 * twos:2]
    margin = jnp.minimum(source_of - 1, reach - receiver)
    moved = jax.random.randint(jax.random.fold_in(own_key, 1), (twos,), 0, 1 << 20) % (margin + 1)
    sizes = sizes.at[1:1 + 2 * twos:2].set(source_of - moved).at[2:2 + 2 * twos:2].set(receiver + moved)
    return sizes[jax.random.permutation(jax.random.fold_in(own_key, 2), count)]


def scatter_about(rng, extent, spread, limit, shards=(), held_as=jnp.bfloat16):
    entries = spread * jax.random.normal(rng, extent, jnp.float32)
    if shards:
        entries = entries * level_of(rng, extent, shards, -0.22, 0.18)
    return jnp.clip(entries, -limit, limit).astype(held_as)


def setup_inputs(seed: int = 0) -> dict:
    key_list = jax.random.split(jax.random.key(seed), 19)
    layer_input = draw_layer_input(jax.random.fold_in(key_list[18], 71), 0)
    doc_lengths = jax.vmap(lambda own: uneven(own, DOCS, SEQ_LEN, DOC_MOST, 1))(jax.random.split(key_list[1], SEQUENCES)).reshape((SEQUENCES, DOCS)).astype(jnp.int32)
    query_weight = scatter_about(key_list[2], (D, D), (D // 2) ** -0.5, 0.3125, ((0, 32),))
    key_weight = scatter_about(key_list[3], (D, D), (D // 2) ** -0.5, 0.3125, ((0, 32),))
    value_weight = scatter_about(key_list[4], (D, D), D ** -0.5, 0.21875, ((0, 32),))
    output_weight = scatter_about(key_list[5], (D, D), (D // 16) ** -0.5, 0.875, ((0, 32),))
    query_bias = scatter_about(key_list[6], (D,), 0.5, 3.0, ((0, 32),))
    value_bias = scatter_about(key_list[7], (D,), 0.5, 3.0, ((0, 32),))
    output_bias = scatter_about(key_list[8], (D,), 0.5, 3.0, ((0, 32),))
    first_gain = jnp.clip(1.0 + 0.1 * jax.random.normal(key_list[9], (D,), jnp.float32), 0.5, 1.5).astype(jnp.bfloat16)
    first_shift = scatter_about(key_list[10], (D,), 0.3, 2.0, ((0, 32),))
    inner_weight = scatter_about(key_list[11], (D, FF), D ** -0.5, 0.21875, ((0, 32),))
    inner_bias = scatter_about(key_list[12], (FF,), 0.5, 3.0, ((0, 32),))
    outer_weight = scatter_about(key_list[13], (FF, D), FF ** -0.5, 0.109375, ((0, 32),))
    outer_bias = scatter_about(key_list[14], (D,), 0.5, 3.0, ((0, 32),))
    second_gain = jnp.clip(1.0 + 0.1 * jax.random.normal(key_list[15], (D,), jnp.float32), 0.5, 1.5).astype(jnp.bfloat16)
    second_shift = scatter_about(key_list[16], (D,), 0.3, 2.0, ((0, 32),))
    output_cotangent = scatter_about(key_list[17], (SEQUENCES, SEQ_LEN, D), 1.0, 6.0, ((0, 4), (1, 8)))
    return dict(layer_input=layer_input, doc_lengths=doc_lengths, query_weight=query_weight, key_weight=key_weight, value_weight=value_weight, output_weight=output_weight, query_bias=query_bias, value_bias=value_bias, output_bias=output_bias, first_gain=first_gain, first_shift=first_shift, inner_weight=inner_weight, inner_bias=inner_bias, outer_weight=outer_weight, outer_bias=outer_bias, second_gain=second_gain, second_shift=second_shift, output_cotangent=output_cotangent)


@jax.custom_vjp
def low(v):
    return lax.optimization_barrier(v.astype(jnp.bfloat16)).astype(jnp.float32)

@jax.custom_vjp
def low_back(v):
    return v

def low_keep(v):
    return (low(v), None)

def low_pass(kept, grad):
    return (grad,)

def back_keep(v):
    return (v, None)

def back_low(kept, grad):
    return (low(grad),)
low.defvjp(low_keep, low_pass)
low_back.defvjp(back_keep, back_low)
exact_mode = lax.Precision.HIGHEST
score_scale = 0.125
norm_eps = 1e-12

def matmul(left, right):
    return jnp.dot(left, right, precision=exact_mode, preferred_element_type=jnp.float32)

def segments_of(places, lengths):
    bounds = jnp.cumsum(lengths, dtype=jnp.int32)[:-1]
    return lax.optimization_barrier(jnp.sum((places[:, None] >= bounds[None, :]).astype(jnp.int32), axis=1))

def layer_norm(resid, gain, shift):
    center = resid - lax.optimization_barrier(jnp.mean(resid, axis=-1, keepdims=True))
    inverse = lax.rsqrt(lax.optimization_barrier(jnp.mean(center * center, axis=-1, keepdims=True)) + norm_eps)
    return center * inverse * gain + shift

def gelu_exact(value):
    return jax.nn.gelu(value, approximate=False)

def forward(params, tokens, seg_ids):
    query_w, key_w, value_w, output_w, query_b, value_b, output_b, gain_one, shift_one, inner_w, inner_b, outer_w, outer_b, gain_two, shift_two = params
    length = tokens.shape[0]
    token_low = low(tokens)
    query = low(low_back(matmul(token_low, query_w) + query_b)).reshape(length, HEADS, HEAD_DIM)
    keys = low(low_back(matmul(token_low, key_w))).reshape(length, HEADS, HEAD_DIM)
    values = low(low_back(matmul(token_low, value_w) + value_b)).reshape(length, HEADS, HEAD_DIM)
    block = math.gcd(length, 512)

    def attend(items):
        query_block, seg_block = items
        raw = jnp.einsum('qhd,khd->hqk', query_block, keys, precision=exact_mode)
        score = low_back(raw * score_scale)
        same = seg_block[:, None] == seg_ids[None, :]
        expo = jnp.where(same[None], jnp.exp(score), 0.0)
        total = lax.optimization_barrier(jnp.sum(expo, axis=-1))
        unnorm = low_back(jnp.einsum('hqk,khd->qhd', low(expo), values, precision=exact_mode))
        return unnorm / jnp.transpose(total)[:, :, None]
    mixed = lax.map(jax.checkpoint(attend), (query.reshape(length // block, block, HEADS, HEAD_DIM), seg_ids.reshape(length // block, block)))
    attn = low(mixed.reshape(length, HEADS * HEAD_DIM))
    branch = low_back(matmul(attn, output_w) + output_b)
    first = layer_norm(tokens + branch, gain_one, shift_one)
    inner = low_back(matmul(low(first), inner_w) + inner_b)
    act = low(gelu_exact(inner))
    outer = low_back(matmul(act, outer_w) + outer_b)
    return layer_norm(first + outer, gain_two, shift_two)

def reference(layer_input, doc_lengths, query_weight, key_weight, value_weight, output_weight, query_bias, value_bias, output_bias, first_gain, first_shift, inner_weight, inner_bias, outer_weight, outer_bias, second_gain, second_shift, output_cotangent):
    params = tuple((item.astype(jnp.float32) for item in (query_weight, key_weight, value_weight, output_weight, query_bias, value_bias, output_bias, first_gain, first_shift, inner_weight, inner_bias, outer_weight, outer_bias, second_gain, second_shift)))
    places = jnp.arange(SEQ_LEN, dtype=jnp.int32)

    def one_sequence(totals, items):
        tokens, lengths, cotangent = items
        seg_ids = segments_of(places, lengths)

        def run(weights, inputs):
            return forward(weights, inputs, seg_ids)
        result, pull = jax.vjp(run, params, tokens.astype(jnp.float32))
        grads, token_grad = pull(cotangent.astype(jnp.float32))
        totals = jax.tree.map(jnp.add, totals, grads)
        return (totals, (result.astype(jnp.bfloat16), token_grad.astype(jnp.bfloat16)))
    zeros = tuple((jnp.zeros(item.shape, jnp.float32) for item in params))
    totals, (outputs, input_grads) = lax.scan(one_sequence, zeros, (layer_input, doc_lengths, output_cotangent))
    return (outputs, input_grads, totals[0], totals[1], totals[2], totals[3], totals[4], totals[5], totals[6], totals[7], totals[8], totals[9], totals[10], totals[11], totals[12], totals[13], totals[14])
```

```python
import math

import jax
import jax.numpy as jnp
from jax import lax
from jax.experimental import pallas as pl
from jax.experimental.pallas import tpu as pltpu
from jax.sharding import PartitionSpec as P

HEADS = 12


score_scale = 0.125
norm_eps = 1e-12


def segments_of(places, lengths):
    bounds = jnp.cumsum(lengths, dtype=jnp.int32)[:-1]
    return jnp.sum((places[:, None] >= bounds[None, :]).astype(jnp.int32), axis=1)


def may_meet(first_segs, second_segs):
    return jnp.logical_and(second_segs[-1] >= first_segs[0], second_segs[0] <= first_segs[-1])


def layer_norm_parts(resid, gain, shift):
    center = resid - jnp.mean(resid, axis=-1, keepdims=True)
    inverse = lax.rsqrt(jnp.mean(center * center, axis=-1, keepdims=True) + norm_eps)
    normed = center * inverse
    return (normed * gain + shift, normed, inverse)


def norm_back(grad, normed, inverse, gain):
    scaled = grad * gain
    return inverse * (
        scaled
        - jnp.mean(scaled, axis=-1, keepdims=True)
        - normed * jnp.mean(scaled * normed, axis=-1, keepdims=True)
    )


def gelu_exact(value):
    return jax.nn.gelu(value, approximate=False)


def plain_dot(left, right):
    return jnp.dot(left, right, preferred_element_type=jnp.float32)


def left_dot(left, right):
    return lax.dot_general(
        left, right, (((0,), (0,)), ((), ())), preferred_element_type=jnp.float32
    )


def right_dot(left, right):
    return lax.dot_general(
        left, right, (((1,), (1,)), ((), ())), preferred_element_type=jnp.float32
    )


def key_block(keys, values, begin, block, heads, width):
    kblk = lax.dynamic_slice_in_dim(keys, begin, block, 0).reshape(block, heads, width)
    vblk = lax.dynamic_slice_in_dim(values, begin, block, 0).reshape(block, heads, width)
    return (kblk, vblk)


def make_forward(query_heads, query_segs, lengths):
    heads = query_heads.shape[1]
    width = query_heads.shape[2]

    def attend(carry, piece, start):
        keys, values = piece
        count = keys.shape[0]
        block = math.gcd(count, 512)

        def step(inner, index):
            begin = index * block
            places = begin + jnp.arange(block, dtype=jnp.int32)
            key_segs = segments_of(places, lengths)

            def compute(state):
                unnorm, total = state
                kblk, vblk = key_block(keys, values, begin, block, heads, width)
                same = query_segs[:, None] == key_segs[None, :]
                score = (
                    jnp.einsum(
                        "qhd,khd->hqk", query_heads, kblk, preferred_element_type=jnp.float32
                    )
                    * score_scale
                )
                expo = jnp.where(same[None], jnp.exp(score), 0.0)
                total = total + jnp.sum(expo, axis=-1)
                unnorm = unnorm + jnp.einsum(
                    "hqk,khd->qhd",
                    expo.astype(jnp.bfloat16),
                    vblk,
                    preferred_element_type=jnp.float32,
                )
                return (unnorm, total)

            inner = lax.cond(may_meet(query_segs, key_segs), compute, lambda state: state, inner)
            return (inner, None)

        carry, _ = lax.scan(step, carry, jnp.arange(count // block, dtype=jnp.int32))
        return carry

    return attend


def make_backward(query_heads, query_segs, lengths, grad_heads, offsets):
    heads = query_heads.shape[1]
    width = query_heads.shape[2]

    def attend_back(carry, piece, start):
        keys, values = piece
        count = keys.shape[0]
        block = math.gcd(count, 512)

        def step(inner, index):
            begin = index * block
            places = begin + jnp.arange(block, dtype=jnp.int32)
            key_segs = segments_of(places, lengths)

            def compute(state):
                kblk, vblk = key_block(keys, values, begin, block, heads, width)
                same = query_segs[:, None] == key_segs[None, :]
                score = (
                    jnp.einsum(
                        "qhd,khd->hqk", query_heads, kblk, preferred_element_type=jnp.float32
                    )
                    * score_scale
                )
                expo = jnp.where(same[None], jnp.exp(score), 0.0)
                dprob = jnp.einsum(
                    "qhd,khd->hqk", grad_heads, vblk, preferred_element_type=jnp.float32
                )
                dscore = (expo * (dprob - offsets[:, :, None])).astype(jnp.bfloat16)
                dquery = state[0] + jnp.einsum(
                    "hqk,khd->qhd", dscore, kblk, preferred_element_type=jnp.float32
                )
                key_part = (
                    jnp.einsum(
                        "hqk,qhd->khd", dscore, query_heads, preferred_element_type=jnp.float32
                    ).reshape(block, heads * width)
                    * score_scale
                )
                value_part = jnp.einsum(
                    "hqk,qhd->khd",
                    expo.astype(jnp.bfloat16),
                    grad_heads,
                    preferred_element_type=jnp.float32,
                ).reshape(block, heads * width)
                dkeys = lax.dynamic_update_slice_in_dim(state[1], key_part, begin, 0)
                dvalues = lax.dynamic_update_slice_in_dim(state[2], value_part, begin, 0)
                return (dquery, dkeys, dvalues)

            inner = lax.cond(may_meet(query_segs, key_segs), compute, lambda state: state, inner)
            return (inner, None)

        carry, _ = lax.scan(step, carry, jnp.arange(count // block, dtype=jnp.int32))
        return carry

    return attend_back


def local(
    layer_input,
    doc_lengths,
    query_weight,
    key_weight,
    value_weight,
    output_weight,
    query_bias,
    value_bias,
    output_bias,
    first_gain,
    first_shift,
    inner_weight,
    inner_bias,
    outer_weight,
    outer_bias,
    second_gain,
    second_shift,
    output_cotangent,
):
    micro = layer_input.shape[0]
    rows = layer_input.shape[1]
    model_width = layer_input.shape[2]
    heads = HEADS
    width = model_width // heads
    hidden_width = inner_weight.shape[1]
    seq_len = rows * lax.axis_size("ctx")
    places = lax.axis_index("ctx") * rows + jnp.arange(rows, dtype=jnp.int32)
    f32 = jnp.float32
    totals = [
        jnp.zeros((model_width, model_width), f32),
        jnp.zeros((model_width, model_width), f32),
        jnp.zeros((model_width, model_width), f32),
        jnp.zeros((model_width, model_width), f32),
        jnp.zeros((model_width,), f32),
        jnp.zeros((model_width,), f32),
        jnp.zeros((model_width,), f32),
        jnp.zeros((model_width,), f32),
        jnp.zeros((model_width,), f32),
        jnp.zeros((model_width, hidden_width), f32),
        jnp.zeros((hidden_width,), f32),
        jnp.zeros((hidden_width, model_width), f32),
        jnp.zeros((model_width,), f32),
        jnp.zeros((model_width,), f32),
        jnp.zeros((model_width,), f32),
    ]
    finals = []
    backs = []
    for index in range(micro):
        attn_set = (
            lax.all_gather(query_weight, ("seq", "ctx"), axis=0, tiled=True),
            lax.all_gather(key_weight, ("seq", "ctx"), axis=0, tiled=True),
            lax.all_gather(value_weight, ("seq", "ctx"), axis=0, tiled=True),
            lax.all_gather(output_weight, ("seq", "ctx"), axis=0, tiled=True),
            lax.all_gather(query_bias, ("seq", "ctx"), axis=0, tiled=True),
            lax.all_gather(value_bias, ("seq", "ctx"), axis=0, tiled=True),
            lax.all_gather(output_bias, ("seq", "ctx"), axis=0, tiled=True),
            lax.all_gather(first_gain, ("seq", "ctx"), axis=0, tiled=True),
            lax.all_gather(first_shift, ("seq", "ctx"), axis=0, tiled=True),
        )
        ffn_set = (
            lax.all_gather(inner_weight, ("seq", "ctx"), axis=0, tiled=True),
            lax.all_gather(inner_bias, ("seq", "ctx"), axis=0, tiled=True),
            lax.all_gather(outer_weight, ("seq", "ctx"), axis=0, tiled=True),
            lax.all_gather(outer_bias, ("seq", "ctx"), axis=0, tiled=True),
            lax.all_gather(second_gain, ("seq", "ctx"), axis=0, tiled=True),
            lax.all_gather(second_shift, ("seq", "ctx"), axis=0, tiled=True),
        )
        query_w, key_w, value_w, output_w, query_b, value_b, output_b, gain_one, shift_one = (
            attn_set
        )
        inner_w, inner_b, outer_w, outer_b, gain_two, shift_two = ffn_set
        gain_one_f = gain_one.astype(f32)
        gain_two_f = gain_two.astype(f32)
        tokens = layer_input[index]
        resid_in = tokens.astype(f32)
        lengths = doc_lengths[index]
        query = (plain_dot(tokens, query_w) + query_b.astype(f32)).astype(jnp.bfloat16)
        keys = plain_dot(tokens, key_w).astype(jnp.bfloat16)
        values = (plain_dot(tokens, value_w) + value_b.astype(f32)).astype(jnp.bfloat16)
        query_heads = query.reshape(rows, heads, width)
        query_segs = segments_of(places, lengths)
        attend = make_forward(query_heads, query_segs, lengths)
        start_carry = (jnp.zeros((rows, heads, width), f32), jnp.zeros((heads, rows), f32))
        whole_keys, whole_values = (
            lax.all_gather(keys, "ctx", axis=0, tiled=True),
            lax.all_gather(values, "ctx", axis=0, tiled=True),
        )
        unnorm, total = attend(start_carry, (whole_keys, whole_values), jnp.int32(0))
        total_rows = jnp.transpose(total)[:, :, None]
        mixed = unnorm / total_rows
        attn = mixed.reshape(rows, model_width).astype(jnp.bfloat16)
        branch = plain_dot(attn, output_w) + output_b.astype(f32)
        first, first_normed, first_inverse = layer_norm_parts(
            resid_in + branch, gain_one_f, shift_one.astype(f32)
        )
        first_low = first.astype(jnp.bfloat16)
        inner = plain_dot(first_low, inner_w) + inner_b.astype(f32)
        act, act_pull = jax.vjp(gelu_exact, inner)
        act_low = act.astype(jnp.bfloat16)
        outer = plain_dot(act_low, outer_w) + outer_b.astype(f32)
        final, second_normed, second_inverse = layer_norm_parts(
            first + outer, gain_two_f, shift_two.astype(f32)
        )
        finals.append(final.astype(jnp.bfloat16))
        back_set = (query_w, key_w, value_w, output_w, gain_one, inner_w, outer_w, gain_two)
        (
            back_query,
            back_key,
            back_value,
            back_output,
            back_gain_one,
            back_inner,
            back_outer,
            back_gain_two,
        ) = back_set
        cotangent = output_cotangent[index].astype(f32)
        totals[13] = totals[13] + jnp.sum(cotangent * second_normed, axis=0)
        totals[14] = totals[14] + jnp.sum(cotangent, axis=0)
        grad_two = norm_back(cotangent, second_normed, second_inverse, back_gain_two.astype(f32))
        grad_outer = grad_two.astype(jnp.bfloat16)
        totals[12] = totals[12] + jnp.sum(grad_outer.astype(f32), axis=0)
        totals[11] = totals[11] + left_dot(act_low, grad_outer)
        grad_act = right_dot(grad_outer, back_outer)
        grad_inner = act_pull(grad_act)[0].astype(jnp.bfloat16)
        totals[10] = totals[10] + jnp.sum(grad_inner.astype(f32), axis=0)
        totals[9] = totals[9] + left_dot(first_low, grad_inner)
        grad_first = grad_two + right_dot(grad_inner, back_inner)
        totals[7] = totals[7] + jnp.sum(grad_first * first_normed, axis=0)
        totals[8] = totals[8] + jnp.sum(grad_first, axis=0)
        grad_one = norm_back(grad_first, first_normed, first_inverse, back_gain_one.astype(f32))
        grad_branch = grad_one.astype(jnp.bfloat16)
        totals[6] = totals[6] + jnp.sum(grad_branch.astype(f32), axis=0)
        totals[3] = totals[3] + left_dot(attn, grad_branch)
        grad_mixed = right_dot(grad_branch, back_output).reshape(rows, heads, width)
        grad_heads = (grad_mixed / total_rows).astype(jnp.bfloat16)
        offsets = jnp.transpose(jnp.sum(grad_mixed * mixed, axis=-1)) / total
        attend_back = make_backward(query_heads, query_segs, lengths, grad_heads, offsets)
        query_zero = jnp.zeros((rows, heads, width), f32)
        back_carry = (
            query_zero,
            jnp.zeros((seq_len, model_width), f32),
            jnp.zeros((seq_len, model_width), f32),
        )
        back_out = attend_back(back_carry, (whole_keys, whole_values), jnp.int32(0))
        dquery = back_out[0]
        own_keys, own_values = (
            lax.psum_scatter(back_out[1], "ctx", scatter_dimension=0, tiled=True),
            lax.psum_scatter(back_out[2], "ctx", scatter_dimension=0, tiled=True),
        )
        grad_query = (dquery.reshape(rows, model_width) * score_scale).astype(jnp.bfloat16)
        grad_keys = own_keys.astype(jnp.bfloat16)
        grad_values = own_values.astype(jnp.bfloat16)
        totals[0] = totals[0] + left_dot(tokens, grad_query)
        totals[1] = totals[1] + left_dot(tokens, grad_keys)
        totals[2] = totals[2] + left_dot(tokens, grad_values)
        totals[4] = totals[4] + jnp.sum(grad_query.astype(f32), axis=0)
        totals[5] = totals[5] + jnp.sum(grad_values.astype(f32), axis=0)
        grad_tokens = (
            grad_one
            + right_dot(grad_query, back_query)
            + right_dot(grad_keys, back_key)
            + right_dot(grad_values, back_value)
        )
        backs.append(grad_tokens.astype(jnp.bfloat16))
    summed = (
        lax.psum_scatter(totals[0], ("seq", "ctx"), scatter_dimension=0, tiled=True),
        lax.psum_scatter(totals[1], ("seq", "ctx"), scatter_dimension=0, tiled=True),
        lax.psum_scatter(totals[2], ("seq", "ctx"), scatter_dimension=0, tiled=True),
        lax.psum_scatter(totals[3], ("seq", "ctx"), scatter_dimension=0, tiled=True),
        lax.psum_scatter(totals[4], ("seq", "ctx"), scatter_dimension=0, tiled=True),
        lax.psum_scatter(totals[5], ("seq", "ctx"), scatter_dimension=0, tiled=True),
        lax.psum_scatter(totals[6], ("seq", "ctx"), scatter_dimension=0, tiled=True),
        lax.psum_scatter(totals[7], ("seq", "ctx"), scatter_dimension=0, tiled=True),
        lax.psum_scatter(totals[8], ("seq", "ctx"), scatter_dimension=0, tiled=True),
        lax.psum_scatter(totals[9], ("seq", "ctx"), scatter_dimension=0, tiled=True),
        lax.psum_scatter(totals[10], ("seq", "ctx"), scatter_dimension=0, tiled=True),
        lax.psum_scatter(totals[11], ("seq", "ctx"), scatter_dimension=0, tiled=True),
        lax.psum_scatter(totals[12], ("seq", "ctx"), scatter_dimension=0, tiled=True),
        lax.psum_scatter(totals[13], ("seq", "ctx"), scatter_dimension=0, tiled=True),
        lax.psum_scatter(totals[14], ("seq", "ctx"), scatter_dimension=0, tiled=True),
    )
    return (jnp.stack(finals), jnp.stack(backs)) + tuple(summed)


MESH = pl.DeviceIdType.MESH


RELS = ("0", "U1", "D1", "U2", "D2", "U3", "D3")
FAR = RELS[1:]
GATHER_SEMS = 320


class Gatherer:
    def __init__(self, refs, sems):
        self.wqkv, self.wmid, self.wlast, self.vecs, self.xall = refs
        self.send_sems, self.recv_sems = sems
        self.z, self.c = lax.axis_index("seq"), lax.axis_index("ctx")
        z, c = self.z, self.c
        self.up, self.down = {"seq": jnp.minimum(z + 1, 3)}, {"seq": jnp.maximum(z - 1, 0)}
        self.xn, self.yn, self.sib = {"ctx": c ^ 2}, {"ctx": c ^ 4}, {"ctx": c ^ 1}
        self.col = {"o": c, "x": c ^ 2, "y": c ^ 4, "d": c ^ 6}
        self.slots, self.drains = {}, []

    def parts(self, group, dev, half=None):
        cols = slice(None) if half is None else pl.ds(384 * half, 384)
        rows = pl.ds(pl.multiple_of(dev * 24, 8), 24)
        if group == "A":
            return [self.wqkv.at[:, rows, cols]] + ([self.vecs.at[dev]] if half != 1 else [])
        if group == "B":
            return [self.wmid.at[:, rows, cols]]
        if group == "Q":
            return [self.wlast.at[pl.ds(pl.multiple_of(dev * 96, 8), 96), cols]]
        return [self.xall.at[:, pl.ds(pl.multiple_of((dev % 8) * 128, 128), 128), cols]]

    def copies(self, key, group, dev, target, half):
        out = []
        for n, ref in enumerate(self.parts(group, dev, half)):
            i = self.slots.setdefault((group, key, n), len(self.slots))
            out.append(pltpu.make_async_remote_copy(
                src_ref=ref, dst_ref=ref, send_sem=self.send_sems.at[i], recv_sem=self.recv_sems.at[i],
                device_id=target, device_id_type=MESH))
        return out

    def emit(self, cond, fn):
        if cond is True:
            fn()
        else:
            def go():
                fn()
            pl.when(cond)(go)

    def zs(self, rel):
        if rel == "0":
            return self.z
        return self.z - int(rel[1]) if rel[0] == "U" else self.z + int(rel[1])

    def valid(self, rel):
        if rel == "0":
            return True
        return self.z >= int(rel[1]) if rel[0] == "U" else self.z + int(rel[1]) <= 3

    def dev(self, rel, col):
        return self.zs(rel) * 8 + self.col[col]

    def send(self, key, group, dev, target, cond, half=None):
        self.emit(cond, lambda: [cp.start() for cp in self.copies(key, group, dev, target, half)])
        self.drains.append((cond, lambda: [cp.wait_send() for cp in self.copies(key, group, dev, target, half)]))

    def recv(self, key, group, dev, cond, half=None):
        self.emit(cond, lambda: [cp.wait_recv() for cp in self.copies(key, group, dev, self.sib, half)])

    def onward(self, group, rel, col):
        z = self.z
        n = 0 if rel == "0" else int(rel[1])
        dev = self.dev(rel, col)
        if rel[0] in "0U" and n < 3:
            self.send(("z" + col, f"U{n + 1}"), group, dev, self.up, jnp.logical_and(z < 3, z >= n))
        if rel[0] in "0D" and n < 3:
            self.send(("z" + col, f"D{n + 1}"), group, dev, self.down, jnp.logical_and(z > 0, z + n <= 3))

    def fan(self, group, rel):
        dev, cond = self.dev(rel, "o"), self.valid(rel)
        self.send(("x", rel), group, dev, self.xn, cond)
        self.send(("y", rel), group, dev, self.yn, cond)

    def sibling(self, group, rel, col):
        self.send(("s" + col, rel), group, self.dev(rel, col), self.sib, self.valid(rel))

    def z_step(self, group, rel, col="o", fan=True):
        self.recv(("z" + col, rel), group, self.dev(rel, col), self.valid(rel))
        self.onward(group, rel, col)
        if fan:
            self.fan(group, rel)
        self.sibling(group, rel, col)

    def plane_step(self, group, rel, onward=False):
        devx, devy, cond = self.dev(rel, "x"), self.dev(rel, "y"), self.valid(rel)
        self.recv(("x", rel), group, devx, cond)
        self.send(("e", rel), group, devx, self.yn, cond, half=0)
        if onward:
            self.onward(group, rel, "x")
        self.sibling(group, rel, "x")
        self.recv(("y", rel), group, devy, cond)
        self.send(("f", rel), group, devy, self.xn, cond, half=1)
        if onward:
            self.onward(group, rel, "y")
        self.sibling(group, rel, "y")

    def diag_step(self, group, rel, onward=False):
        devd, cond = self.dev(rel, "d"), self.valid(rel)
        self.recv(("e", rel), group, devd, cond, half=0)
        self.recv(("f", rel), group, devd, cond, half=1)
        if onward:
            self.onward(group, rel, "d")
        self.sibling(group, rel, "d")

    def finish(self, group, rels=RELS):
        for rel in rels:
            for col in "oxyd":
                self.recv(("s" + col, rel), group, self.zs(rel) * 8 + (self.col[col] ^ 1), self.valid(rel))

    def barrier(self):
        barrier = pltpu.get_barrier_semaphore()
        for t in (self.xn, self.yn, self.sib):
            pl.semaphore_signal(barrier, inc=1, device_id=t, device_id_type=MESH)
        for n in range(1, 4):
            pl.semaphore_signal(barrier, inc=1, device_id={"seq": (self.z + n) & 3}, device_id_type=MESH)
        pl.semaphore_wait(barrier, 6)

    def drain(self):
        assert len(self.slots) <= GATHER_SEMS
        for cond, fn in self.drains:
            self.emit(cond, fn)


def gather_kernel(q, k, v, o, win, wout, vec, x, wqkv, wmid, wlast, vecs, xall, send_sems, recv_sems, own_sems):
    g = Gatherer((wqkv, wmid, wlast, vecs, xall), (send_sems, recv_sems))
    z, c = g.z, g.c
    d = z * 8 + c
    own = []

    def local(src, dst):
        cp = pltpu.make_async_copy(src, dst, own_sems.at[len(own)])
        cp.start()
        own.append(cp)

    rows = pl.ds(pl.multiple_of(d * 24, 8), 24)
    local(q, wqkv.at[0, rows]); local(k, wqkv.at[1, rows]); local(v, wqkv.at[2, rows])
    local(vec, vecs.at[d])
    local(x, xall.at[:, pl.ds(pl.multiple_of(c * 128, 128), 128)])
    local(o, wmid.at[0, rows])
    for b in range(4):
        local(win.at[:, pl.ds(768 * b, 768)], wmid.at[1 + b, rows])
    local(wout, wlast.at[pl.ds(pl.multiple_of(d * 96, 8), 96)])
    g.barrier()
    for cp in own:
        cp.wait()
    gather_schedule(g)
    g.drain()


def gather_schedule(g):
    g.onward("A", "0", "o"); g.fan("A", "0"); g.fan("X", "0")
    g.onward("Q", "0", "o")
    g.sibling("A", "0", "o"); g.sibling("X", "0", "o")
    g.fan("Q", "0"); g.sibling("Q", "0", "o")
    g.plane_step("A", "0")
    g.z_step("A", "U1"); g.z_step("A", "D1")
    g.z_step("A", "U2"); g.z_step("A", "D2")
    g.onward("B", "0", "o")
    g.z_step("A", "U3"); g.z_step("A", "D3")
    g.plane_step("X", "0")
    g.fan("B", "0"); g.sibling("B", "0", "o")
    g.plane_step("Q", "0", onward=True)
    for rel in FAR:
        g.plane_step("A", rel)
    for rel in ("U1", "D1"):
        g.z_step("B", rel)
    for rel in RELS:
        g.diag_step("A", rel)
    g.diag_step("X", "0")
    g.diag_step("Q", "0", onward=True)
    for rel in ("U2", "D2"):
        g.z_step("B", rel)
    for rel in ("U1", "D1"):
        for col in "oxyd":
            g.z_step("Q", rel, col, fan=False)
    for rel in ("U3", "D3"):
        g.z_step("B", rel)
    g.plane_step("B", "0")
    for rel in ("U1", "D1"):
        g.plane_step("B", rel)
    for rel in ("U2", "D2"):
        for col in "oxyd":
            g.z_step("Q", rel, col, fan=False)
    for rel in ("U2", "D2", "U3", "D3"):
        g.plane_step("B", rel)
    for rel in ("U3", "D3"):
        for col in "oxyd":
            g.z_step("Q", rel, col, fan=False)
    for rel in RELS:
        g.diag_step("B", rel)
    for group in "AXBQ":
        g.finish(group, ("0",) if group == "X" else RELS)


def gather_all(q, k, v, o, win, wout, vec, x):
    bf = jnp.bfloat16
    sd = jax.ShapeDtypeStruct
    n = GATHER_SEMS
    return pl.pallas_call(
        gather_kernel,
        out_shape=(sd((3, 768, 768), bf), sd((5, 768, 768), bf), sd((3072, 768), bf), sd((32, 16, 128), bf), sd((3, 1024, 768), bf)),
        in_specs=[pl.BlockSpec(memory_space=pltpu.VMEM)] * 8,
        out_specs=tuple([pl.BlockSpec(memory_space=pl.ANY)] * 5),
        scratch_shapes=[pltpu.SemaphoreType.DMA((n,)), pltpu.SemaphoreType.DMA((n,)), pltpu.SemaphoreType.DMA((11,))],
        compiler_params=pltpu.CompilerParams(collective_id=1, has_side_effects=True),
        name="gather_all",
    )(q, k, v, o, win, wout, vec, x)


REDUCE_SEMS = 224
REUSED = {9: 0, 11: 2, 10: 1}
REDUCE_ORDER = (
    ("P", 2), ("P", 8), ("P", 1), ("P", 7), ("P", 4), ("SA", 2), ("CH", "q", 2, 0, 2), ("P", 5), ("P", 6), ("P", 0),
    ("SA", 7), ("P", 3), ("CH", "q", 2, 0, 1), ("SA", 1), ("SP", 0, 1), ("SA", 6), ("SA", 5), ("SA", 8), ("SA", 4),
    ("D", "b", 2), ("D", "b", 0), ("CH", "q", 2, 1, 2), ("SP", 2, 0), ("SA", 0), ("CH", "q", 2, 0, 3),
    ("CH", "q", 2, 1, 1), ("XA", 0, 1), ("CH", "q", 1, 0, 3), ("D", "b", 1), ("D", "b", 3), ("P", 11),
    ("PL", "b", 1, 0), ("CH", "q", 1, 0, 2), ("PL", "b", 0, 1), ("PL", "b", 2, 0), ("PL", "b", 1, 1),
    ("CH", "q", 2, 0, 0), ("CH", "q", 0, 1, 1), ("PL", "b", 0, 0), ("PL", "b", 3, 1), ("SP", 0, 2), ("PL", "b", 2, 1),
    ("P", 9), ("CH", "q", 0, 1, 3), ("PL", "b", 3, 0), ("P", 10), ("XA", 0, 2), ("CH", "q", 0, 1, 0), ("D", "x", 1),
    ("SA", 11), ("SP", 0, 0), ("OW", "b", 2, 0), ("SA", 9), ("SA", 10), ("SA", 3), ("D", "a", 3), ("CH", "q", 1, 0, 0),
    ("XA", 0, 0), ("CH", "q", 0, 1, 2), ("CH", "q", 1, 1, 3), ("CH", "q", 2, 1, 3), ("D", "a", 2), ("D", "a", 0),
    ("D", "a", 1), ("D", "x", 0), ("CH", "q", 3, 0, 2), ("D", "x", 2), ("CH", "q", 1, 1, 0), ("SP", 1, 0), ("SP", 1, 1),
    ("PL", "a", 3, 0), ("PL", "a", 3, 1), ("XA", 2, 0), ("CH", "q", 3, 0, 0), ("PL", "a", 2, 1), ("CH", "q", 1, 1, 2),
    ("SP", 2, 1), ("PL", "a", 0, 0), ("SP", 3, 2), ("OW", "b", 2, 1), ("CH", "q", 3, 0, 3), ("CH", "b", 2, 1, 0),
    ("PL", "a", 1, 1), ("SP", 1, 2), ("XA", 1, 0), ("PL", "x", 0, 0), ("PL", "a", 0, 1), ("PL", "x", 0, 1),
    ("PL", "a", 1, 0), ("SP", 2, 2), ("OW", "b", 1, 0), ("XA", 1, 2), ("CH", "q", 3, 0, 1), ("SP", 3, 0), ("XA", 2, 1),
    ("OW", "b", 3, 1), ("OW", "b", 0, 0), ("AR", "q", 1, 3), ("CH", "q", 1, 1, 1), ("PL", "a", 2, 0), ("OW", "b", 0, 1),
    ("OW", "b", 3, 0), ("CH", "b", 3, 0, 0), ("XA", 3, 0), ("AR", "q", 0, 2), ("XA", 2, 2), ("PL", "x", 2, 1),
    ("XA", 1, 1), ("PL", "x", 1, 0), ("OW", "a", 3, 0), ("OW", "b", 1, 1), ("OW", "a", 2, 1), ("OW", "a", 3, 1),
    ("CH", "a", 3, 0, 0), ("CH", "b", 2, 0, 0), ("CH", "q", 2, 1, 0), ("AR", "q", 0, 3), ("D", "q", 0),
    ("CH", "b", 0, 1, 0), ("CH", "b", 1, 0, 0), ("PL", "x", 1, 1), ("PL", "x", 2, 0), ("SP", 3, 1), ("AR", "q", 1, 0),
    ("OW", "a", 0, 0), ("AR", "q", 1, 1), ("OW", "a", 0, 1), ("CH", "q", 1, 0, 1), ("CH", "a", 0, 1, 0),
    ("AR", "q", 1, 2), ("OW", "a", 1, 1), ("XA", 3, 2), ("OW", "x", 0, 0), ("OW", "a", 1, 0), ("OW", "a", 2, 0),
    ("CH", "a", 1, 1, 0), ("AR", "q", 0, 1), ("AR", "q", 0, 0), ("PL", "q", 0, 1), ("PL", "q", 0, 0),
    ("CH", "a", 1, 0, 0), ("CH", "a", 2, 0, 0), ("OW", "x", 2, 1), ("OW", "x", 0, 1), ("XA", 3, 1),
    ("CH", "b", 1, 1, 0), ("OW", "x", 1, 1), ("BASE",), ("OW", "x", 1, 0), ("OW", "x", 2, 0), ("AR", "b", 0, 0),
    ("CH", "a", 2, 1, 0), ("AR", "a", 1, 0), ("AR", "b", 1, 0), ("OW", "q", 0, 1), ("OW", "q", 0, 0), ("AR", "a", 0, 0),
)
SPAN = {"q": (0, 4), "b": (4, 5), "a": (9, 3)}


def reduce_kernel(act, gi, first_low, g_outer, attn, g_branch, tokens, dq, xall, dk, dv, wqkv, dr1, vg,
                  oq, oo, oin, oout, ox, ovec,
                  p0, p1, p2, small, wbuf, base, run, out_buf, land, rx, tx, lx,
                  db, da, dqq, dxx, pb, pa, pq, px, ub, ua, uq, full, sx, vl, load_sems, send_sems, recv_sems):
    z = lax.axis_index("seq")
    c = lax.axis_index("ctx")
    chip, core = c >> 1, c & 1
    up, down = {"seq": jnp.minimum(z + 1, 3)}, {"seq": jnp.maximum(z - 1, 0)}
    xn, yn, sib = {"ctx": c ^ 2}, {"ctx": c ^ 4}, {"ctx": c ^ 1}
    bf, f32 = jnp.bfloat16, jnp.float32
    bases, size = {}, [0]
    loads = {}

    def load(name, src, dst):
        cp = pltpu.make_async_copy(src, dst, load_sems.at[len(loads)])
        cp.start()
        loads[name] = cp

    waited = set()

    def need(*names):
        for name in names:
            if name not in waited:
                waited.add(name)
                loads[name].wait()

    for m in range(4):
        load(f"act{m}", act.at[:, pl.ds(768 * m, 768)], p1.at[pl.ds(384 * m, 384)])
    load("go", g_outer, small.at[0])
    load("at", attn, small.at[1])
    load("gb", g_branch, small.at[2])
    load("fl", first_low, small.at[3])
    for m in range(4):
        load(f"gi{m}", gi.at[:, pl.ds(768 * m, 768)], p1.at[pl.ds(1536 + 384 * m, 384)])
    load("tok", tokens, small.at[4])
    load("dq", dq, small.at[5])
    load("x", xall, p0)
    load("dv", dv, p2)
    load("w", wqkv, wbuf)
    load("r", dr1, base)

    barrier = pltpu.get_barrier_semaphore()
    for t in (xn, yn, sib):
        pl.semaphore_signal(barrier, inc=1, device_id=t, device_id_type=MESH)
    for n in range(1, 4):
        pl.semaphore_signal(barrier, inc=1, device_id={"seq": (z + n) & 3}, device_id_type=MESH)
    pl.semaphore_wait(barrier, 6)

    def slot(name, count=1):
        if name not in bases:
            bases[name] = size[0]
            size[0] += count
        return bases[name]

    def copy(src, dst, index, target):
        return pltpu.make_async_remote_copy(
            src_ref=src, dst_ref=dst, send_sem=send_sems.at[index], recv_sem=recv_sems.at[index],
            device_id=target, device_id_type=MESH)

    mine = pl.ds(pl.multiple_of(core * 384, 128), 384)
    other = pl.ds(pl.multiple_of((1 - core) * 384, 128), 384)

    def add_into(dst, src):
        if len(dst.shape) == 2:
            dst[...] = (dst[...].astype(f32) + src[...].astype(f32)).astype(bf)
        else:
            def go(m, _):
                dst[m] = (dst[m].astype(f32) + src[m].astype(f32)).astype(bf)
                return 0
            lax.fori_loop(0, dst.shape[0], go, 0)

    def product(m, t, lhs, rhs):
        def go(i, _):
            block = lhs[:, pl.ds(pl.multiple_of(i * 384, 128), 384)]
            at = pl.ds(i * 8, 8)
            run[m, at] = left_dot(block, rhs[:, mine]).reshape(8, 48, 384).astype(bf)
            out_buf[t, at] = left_dot(block, rhs[:, other]).reshape(8, 48, 384).astype(bf)
            return 0
        lax.fori_loop(0, 2, go, 0)
        s_copy(m, t).start()

    def s_copy(m, t):
        return copy(out_buf.at[t], land.at[m], slot(("s", m)), sib)

    def s_add(m, t):
        s_copy(m, t).wait_recv()
        add_into(run.at[m], land.at[m])

    def share(name, zs, ch):
        if name == "q":
            return run.at[zs, pl.ds(ch * 4, 4)]
        if name == "x":
            return rx.at[ch]
        lo, n = SPAN[name]
        return run.at[pl.ds(lo, n), zs * 4 + ch]

    def half(ref, n):
        rows = ref.shape[-2] // 2
        return ref.at[:, pl.ds(rows * n, rows)]

    lands = {"b": (db, pb, ub), "a": (da, pa, ua), "q": (dqq, pq, uq), "x": (dxx, px, None)}
    wide = {"b": True, "a": True, "q": False, "x": False}

    def zs_of(name, i):
        return i if wide[name] else z

    def d_copy(name, i, n):
        if name == "x":
            rows = pl.ds(128 * n, 128)
            return copy(rx.at[chip ^ 3, i, rows], dxx.at[n, i], slot(("d", name, i, n)), (yn, xn)[n])
        return copy(half(share(name, zs_of(name, i), chip ^ 3), n), lands[name][0].at[n, i], slot(("d", name, i, n)), (yn, xn)[n])

    def p_copy(name, i, n):
        if name == "x":
            return copy(rx.at[chip ^ (n + 1), i], px.at[n, i], slot(("p", name, i, n)), (xn, yn)[n])
        return copy(share(name, zs_of(name, i), chip ^ (n + 1)), lands[name][1].at[n, i], slot(("p", name, i, n)), (xn, yn)[n])

    def diag(name, i):
        d_copy(name, i, 0).start()
        d_copy(name, i, 1).start()

    def plane(name, i, n):
        d_copy(name, i, n).wait_recv()
        if name == "x":
            add_into(rx.at[chip ^ (n + 1), i, pl.ds(128 * n, 128)], dxx.at[n, i])
        else:
            add_into(half(share(name, zs_of(name, i), chip ^ (n + 1)), n), lands[name][0].at[n, i])
        p_copy(name, i, n).start()

    def own(name, i, n):
        p_copy(name, i, n).wait_recv()
        if name == "x":
            add_into(rx.at[chip, i], px.at[n, i])
        else:
            add_into(share(name, zs_of(name, i), chip), lands[name][1].at[n, i])

    def cols_of(name):
        return range(4) if name == "q" else range(1)

    def u_copy(name, t, n, col):
        place = t - 1 if n == 0 else t
        return copy(share(name, t, chip ^ col), lands[name][2].at[n, place, col], slot(("u", name, n, col), 3) + place, (up, down)[n])

    def chain(name, t, n, col):
        def go():
            def take():
                u_copy(name, t, n, col).wait_recv()
                add_into(share(name, t, chip ^ col), lands[name][2].at[n, t - 1 if n == 0 else t, col])
            pl.when(z > 0 if n == 0 else z < 3)(take)
            u_copy(name, t, n, col).start()
        pl.when(z < t if n == 0 else z > t)(go)

    def arrive(name, n, col):
        def take():
            u_copy(name, z, n, col).wait_recv()
            add_into(share(name, z, chip ^ col), lands[name][2].at[n, z - 1 if n == 0 else z, col])
        pl.when(z > 0 if n == 0 else z < 3)(take)

    def x_copy(i, s):
        ch = chip ^ (3, 1, 2, 0)[i]
        return copy(tx.at[ch, s], lx.at[ch, s], slot(("sx", i, s)), sib)

    def spread(i, s):
        ch = chip ^ (3, 1, 2, 0)[i]
        need("dk", "dv", "w")
        rows = pl.ds(pl.multiple_of(s * 1024 + ch * 256, 256), 256)
        kr, vr = p1[rows, :], p2[rows, :]
        m_rows = pl.ds(pl.multiple_of(core * 384, 128), 384)
        o_rows = pl.ds(pl.multiple_of((1 - core) * 384, 128), 384)
        tx[ch, s] = (right_dot(kr, wbuf[1, o_rows]) + right_dot(vr, wbuf[2, o_rows])).astype(bf)
        x_copy(i, s).start()
        rx[ch, s] = (right_dot(kr, wbuf[1, m_rows]) + right_dot(vr, wbuf[2, m_rows])).astype(bf)

    def x_add(i, s):
        ch = chip ^ (3, 1, 2, 0)[i]
        x_copy(i, s).wait_recv()
        add_into(rx.at[ch, s], lx.at[ch, s])

    v_to = [sib, xn, yn]

    def v_copy(n):
        return copy(vl.at[0], vl.at[n + 1], slot(("v", n)), v_to[n])

    def v_step(n):
        v_copy(n).wait()
        vl[0] = vl[0] + vl[n + 1]
        if n < 2:
            v_copy(n + 1).start()

    def vz_copy(n):
        return copy(vl.at[0], vl.at[3 + n], slot(("vz", n)), {"seq": (z + n) & 3})

    first_blocks = set(range(9))

    def block(m):
        if m < 4:
            need(f"act{m}", "go")
            product(m, m, p1.at[pl.ds(384 * m, 384)], small.at[0])
        elif m == 4:
            need("at", "gb")
            product(m, m, small.at[1], small.at[2])
        elif m < 9:
            need("fl", f"gi{m - 5}")
            product(m, m, small.at[3], p1.at[pl.ds(1536 + 384 * (m - 5), 384)])
        else:
            s_copy(REUSED[m], REUSED[m]).wait_send()
            if m == 9:
                need("tok", "dq")
                product(m, 0, small.at[4], small.at[5])
            elif m == 11:
                need("x", "dv")
                product(m, 2, p0, p2)
            else:
                need("x", "dk")
                product(m, 1, p0, p1)

        first_blocks.discard(m)
        if not first_blocks and "dk" not in loads:
            load("dk", dk, p1)

    def own_rows():
        need("r", "w", "dq")
        base[...] += right_dot(small[5], wbuf[0])

    sib_rows, my_rows = pl.ds(pl.multiple_of((1 - core) * 24, 8), 24), pl.ds(pl.multiple_of(core * 24, 8), 24)
    ends = []

    def end(src, dst, name):
        cp = copy(src, dst, slot(name), sib)
        cp.start()
        ends.append(cp)

    def x_end(s):
        return copy(rx.at[chip, s, pl.ds(pl.multiple_of((1 - core) * 128, 8), 128)], sx.at[s], slot(("fx", s)), sib)

    def close(name, s=0):
        if name == "x":
            x_end(s).start()
            return
        lo, n = SPAN[name]
        me = share(name, z, chip)
        for m in range(n):
            full[lo + m] = me[m].astype(f32)
        if name == "b":
            end(full.at[4, sib_rows], oo.at[:, mine], ("f", "o"))
            for m in range(4):
                at = pl.ds(pl.multiple_of(768 * m + core * 384, 128), 384)
                end(full.at[5 + m, sib_rows], oin.at[:, at], ("f", "i", m))
                oin[:, at] = full[5 + m, my_rows]
            oo[:, mine] = full[4, my_rows]
        elif name == "q":
            end(full.at[pl.ds((1 - core) * 2, 2)], oout.at[:, :, mine], ("f", "q"))
            for m in range(2):
                oout[m, :, mine] = full[core * 2 + m]
        else:
            end(full.at[pl.ds(9, 3), sib_rows], oq.at[:, :, mine], ("f", "a"))
            for m in range(3):
                oq[m, :, mine] = full[9 + m, my_rows]

    run_step = {
        "P": block, "SA": lambda m: s_add(m, REUSED.get(m, m)), "SP": spread, "XA": x_add, "D": diag, "PL": plane, "OW": own,
        "CH": chain, "AR": arrive, "BASE": own_rows}
    lasts = {}
    for at, step in enumerate(REDUCE_ORDER):
        if step[0] == "OW" and step[1] in "xq":
            lasts[(step[1], step[2])] = at
        elif step[0] == "AR" and step[1] in "ba":
            lasts[(step[1], 0)] = at
    closing = {at: key for key, at in lasts.items()}
    vec_at = {len(REDUCE_ORDER) * n // 8: n - 2 for n in (2, 3, 4)}
    vl[0] = vg[...]
    v_copy(0).start()
    for at, step in enumerate(REDUCE_ORDER):
        run_step[step[0]](*step[1:])
        if at in closing:
            close(*closing[at])
        if at in vec_at:
            v_step(vec_at[at])
            if vec_at[at] == 2:
                for n in range(1, 4):
                    vz_copy(n).start()

    for n in range(1, 4):
        vz_copy(n).wait()
    whole = vl[0] + vl[4] + vl[5] + vl[6]
    first = pltpu.roll(whole, lax.rem(768 - 24 * (z * 8 + c), 768), 1)[0:8, 0:128]
    second = pltpu.roll(whole, lax.rem(768 - 96 * c, 768), 1)[8:16, 0:128]
    picked = jnp.sum(jnp.where(lax.broadcasted_iota(jnp.int32, (8, 128), 0) == z, second, 0.0), axis=0, keepdims=True)
    ovec[0:8] = first
    ovec[8:16] = jnp.broadcast_to(picked, (8, 128))
    for s in range(3):
        tok = pl.ds(128 * s, 128)
        ox[s, :, mine] = (rx[chip, s, pl.ds(pl.multiple_of(core * 128, 8), 128)].astype(f32) + base[tok, mine]).astype(bf)
        x_end(s).wait()
        ox[s, :, other] = (sx[s].astype(f32) + base[tok, other]).astype(bf)
    for cp in ends:
        cp.wait()
    for step in REDUCE_ORDER:
        if step[0] == "P":
            if step[1] >= 9 or step[1] not in REUSED.values():
                s_copy(step[1], REUSED.get(step[1], step[1])).wait_send()
        elif step[0] == "SP":
            x_copy(*step[1:]).wait_send()
        elif step[0] == "D":
            d_copy(*step[1:], 0).wait_send()
            d_copy(*step[1:], 1).wait_send()
        elif step[0] == "PL":
            p_copy(*step[1:]).wait_send()
        elif step[0] == "CH":
            name, t, n, col = step[1:]
            pl.when(z < t if n == 0 else z > t)(lambda: u_copy(name, t, n, col).wait_send())
    assert size[0] <= REDUCE_SEMS


def reduce_all(act, gi, first_low, g_outer, attn, g_branch, tokens, dq, xall, dk, dv, wqkv, dr1, vg):
    bf, f32 = jnp.bfloat16, jnp.float32
    sd = jax.ShapeDtypeStruct
    vm, hbm = pl.BlockSpec(memory_space=pltpu.VMEM), pl.BlockSpec(memory_space=pl.ANY)
    v = pltpu.VMEM
    scratch = [
        v((3072, 768), bf), v((3072, 768), bf), v((3072, 768), bf), v((6, 384, 768), bf), v((3, 768, 768), bf), v((384, 768), f32),
        v((12, 16, 48, 384), bf), v((9, 16, 48, 384), bf), v((12, 16, 48, 384), bf),
        v((4, 3, 256, 384), bf), v((4, 3, 256, 384), bf), v((4, 3, 256, 384), bf),
        v((2, 4, 5, 24, 384), bf), v((2, 4, 3, 24, 384), bf), v((2, 1, 4, 24, 384), bf), v((2, 3, 128, 384), bf),
        v((2, 4, 5, 48, 384), bf), v((2, 4, 3, 48, 384), bf), v((2, 1, 4, 48, 384), bf), v((2, 3, 256, 384), bf),
        v((2, 3, 1, 5, 48, 384), bf), v((2, 3, 1, 3, 48, 384), bf), v((2, 3, 4, 4, 48, 384), bf),
        v((12, 48, 384), f32), v((3, 128, 384), bf), v((7, 16, 768), f32),
        pltpu.SemaphoreType.DMA((24,)), pltpu.SemaphoreType.DMA((REDUCE_SEMS,)), pltpu.SemaphoreType.DMA((REDUCE_SEMS,)),
    ]
    return pl.pallas_call(
        reduce_kernel,
        out_shape=(sd((3, 24, 768), f32), sd((24, 768), f32), sd((24, 3072), f32), sd((2, 48, 768), f32),
                   sd((3, 128, 768), bf), sd((16, 128), f32)),
        in_specs=[hbm] * 13 + [vm],
        out_specs=(vm,) * 6,
        scratch_shapes=scratch,
        compiler_params=pltpu.CompilerParams(collective_id=2, has_side_effects=True, vmem_limit_bytes=67000000),
        name="reduce_all",
    )(act, gi, first_low, g_outer, attn, g_branch, tokens, dq, xall, dk, dv, wqkv, dr1, vg)


def stacked(pair, left):
    zero = jnp.zeros_like(pair)
    return jnp.concatenate([jnp.where(left, pair, zero), jnp.where(left, zero, pair)], axis=0)


def attend_kernel(bounds, q, k, v, qseg, kseg, mixed, total, acc, sums):
    f32, bf = jnp.float32, jnp.bfloat16
    s = pl.program_id(0)
    rows = q.shape[1]
    pairs = q.shape[2] // 128
    left = lax.broadcasted_iota(jnp.int32, (rows, 128), 1) < 64
    acc[...] = jnp.zeros_like(acc)
    sums[...] = jnp.zeros_like(sums)
    segs = jnp.concatenate([qseg[0], qseg[0]], axis=0)

    def block(kb, carry):
        at = pl.ds(pl.multiple_of(kb * KEYS, KEYS), KEYS)
        same = segs == kseg[0, :, at]
        for p in range(pairs):
            cols = slice(128 * p, 128 * p + 128)
            qs = stacked(q[0, :, cols], left) * bf(score_scale)
            score = right_dot(qs, k[0, at, cols])
            expo = jnp.where(same, jnp.exp(score), 0.0)
            part = expo[:, 0:128]
            for n in range(1, KEYS // 128):
                part = part + expo[:, 128 * n:128 * n + 128]
            sums[p] += part
            acc[p] += plain_dot(expo.astype(bf), v[0, at, cols])
        return carry

    lax.fori_loop(bounds[2 * s], bounds[2 * s + 1], block, 0)
    for p in range(pairs):
        row_sum = jnp.broadcast_to(jnp.sum(sums[p], axis=1, keepdims=True), (2 * rows, 128))
        total[0, p] = row_sum
        out = acc[p] / row_sum
        mixed[0, :, 128 * p:128 * p + 128] = jnp.where(left, out[:rows], out[rows:])


def attend_back_kernel(bounds, q, k, v, qseg, kseg, mixed, total, dm, dq, dk, dv, acc, us, cs):
    f32, bf = jnp.float32, jnp.bfloat16
    s = pl.program_id(0)
    rows = q.shape[1]
    pairs = q.shape[2] // 128
    left = lax.broadcasted_iota(jnp.int32, (rows, 128), 1) < 64
    acc[...] = jnp.zeros_like(acc)
    dk[...] = jnp.zeros_like(dk)
    dv[...] = jnp.zeros_like(dv)
    segs = jnp.concatenate([qseg[0], qseg[0]], axis=0)
    for p in range(pairs):
        cols = slice(128 * p, 128 * p + 128)
        grad = stacked(dm[0, :, cols], left)
        both = jnp.concatenate([mixed[0, :, cols], mixed[0, :, cols]], axis=0)
        us[p] = (grad / total[0, p]).astype(bf)
        cs[p] = jnp.broadcast_to(jnp.sum(grad * both, axis=1, keepdims=True), (2 * rows, 128)) / total[0, p]

    def block(kb, carry):
        at = pl.ds(pl.multiple_of(kb * KEYS, KEYS), KEYS)
        same = segs == kseg[0, :, at]
        for p in range(pairs):
            cols = slice(128 * p, 128 * p + 128)
            qs = stacked(q[0, :, cols], left) * bf(score_scale)
            score = right_dot(qs, k[0, at, cols])
            expo = jnp.where(same, jnp.exp(score), 0.0)
            dprob = right_dot(us[p], v[0, at, cols])
            off = jnp.concatenate([cs[p]] * (KEYS // 128), axis=1)
            dscore = (expo * (dprob - off)).astype(bf)
            acc[p] += plain_dot(dscore, k[0, at, cols])
            dk[0, at, cols] = left_dot(dscore, qs).astype(bf)
            dv[0, at, cols] = left_dot(expo.astype(bf), us[p]).astype(bf)
        return carry

    lax.fori_loop(bounds[2 * s], bounds[2 * s + 1], block, 0)
    for p in range(pairs):
        out = acc[p] * score_scale
        dq[0, :, 128 * p:128 * p + 128] = jnp.where(left, out[:rows], out[rows:]).astype(bf)


KEYS = 256


def attend(bounds, q, k, v, qseg, kseg):
    seqs, rows, width = q.shape
    keys = k.shape[1]
    pairs = width // 128
    f32 = jnp.float32
    sd = jax.ShapeDtypeStruct
    row = lambda n: pl.BlockSpec((1, n, width), lambda s, b: (s, 0, 0))
    return pl.pallas_call(
        attend_kernel,
        out_shape=(sd((seqs, rows, width), f32), sd((seqs, pairs, 2 * rows, 128), f32)),
        grid_spec=pltpu.PrefetchScalarGridSpec(
            num_scalar_prefetch=1, grid=(seqs,),
            in_specs=[row(rows), row(keys), row(keys), pl.BlockSpec((1, rows, 1), lambda s, b: (s, 0, 0)),
                      pl.BlockSpec((1, 1, keys), lambda s, b: (s, 0, 0))],
            out_specs=(row(rows), pl.BlockSpec((1, pairs, 2 * rows, 128), lambda s, b: (s, 0, 0, 0))),
            scratch_shapes=[pltpu.VMEM((pairs, 2 * rows, 128), f32), pltpu.VMEM((pairs, 2 * rows, 128), f32)]),
        compiler_params=pltpu.CompilerParams(dimension_semantics=("arbitrary",), vmem_limit_bytes=60000000),
        name="attend",
    )(bounds, q, k, v, qseg, kseg)


def attend_back(bounds, q, k, v, qseg, kseg, mixed, total, dm):
    seqs, rows, width = q.shape
    keys = k.shape[1]
    pairs = width // 128
    f32, bf = jnp.float32, jnp.bfloat16
    sd = jax.ShapeDtypeStruct
    row = lambda n: pl.BlockSpec((1, n, width), lambda s, b: (s, 0, 0))
    tot = pl.BlockSpec((1, pairs, 2 * rows, 128), lambda s, b: (s, 0, 0, 0))
    return pl.pallas_call(
        attend_back_kernel,
        out_shape=(sd((seqs, rows, width), bf), sd((seqs, keys, width), bf), sd((seqs, keys, width), bf)),
        grid_spec=pltpu.PrefetchScalarGridSpec(
            num_scalar_prefetch=1, grid=(seqs,),
            in_specs=[row(rows), row(keys), row(keys), pl.BlockSpec((1, rows, 1), lambda s, b: (s, 0, 0)),
                      pl.BlockSpec((1, 1, keys), lambda s, b: (s, 0, 0)), row(rows), tot, row(rows)],
            out_specs=(row(rows), row(keys), row(keys)),
            scratch_shapes=[pltpu.VMEM((pairs, 2 * rows, 128), f32), pltpu.VMEM((pairs, 2 * rows, 128), bf),
                            pltpu.VMEM((pairs, 2 * rows, 128), f32)]),
        compiler_params=pltpu.CompilerParams(dimension_semantics=("arbitrary",), vmem_limit_bytes=60000000),
        name="attend_back",
    )(bounds, q, k, v, qseg, kseg, mixed, total, dm)


def place_kernel(oq, oo, oin, oout, ox, gq, gk, gv, go, gin, gout, gx):
    gq[...], gk[...], gv[...] = oq[0], oq[1], oq[2]
    go[...] = oo[...]
    gin[...] = oin[...]
    gout[0:48], gout[48:96] = oout[0], oout[1]
    gx[...] = ox[...]


def place(oq, oo, oin, oout, ox):
    f32 = jnp.float32
    sd = jax.ShapeDtypeStruct
    vm = pl.BlockSpec(memory_space=pltpu.VMEM)
    return pl.pallas_call(
        place_kernel,
        out_shape=(sd((24, 768), f32),) * 4 + (sd((24, 3072), f32), sd((96, 768), f32), sd((3, 128, 768), jnp.bfloat16)),
        in_specs=[vm] * 5, out_specs=(vm,) * 7, name="place",
    )(oq, oo, oin, oout, ox)


def local_fast(
    layer_input, doc_lengths, query_weight, key_weight, value_weight, output_weight, query_bias, value_bias, output_bias,
    first_gain, first_shift, inner_weight, inner_bias, outer_weight, outer_bias, second_gain, second_shift, output_cotangent,
):
    f32, bf = jnp.float32, jnp.bfloat16
    seqs, rows, width = layer_input.shape
    keys = rows * lax.axis_size("ctx")
    tokens_all = seqs * rows
    small = jnp.stack([query_bias, value_bias, output_bias, first_gain, first_shift, outer_bias, second_gain, second_shift])
    vec = jnp.concatenate([jnp.pad(small, ((0, 0), (0, 104))), jnp.pad(inner_bias[None], ((0, 7), (0, 32)))])
    wqkv, wmid, wlast, vecs, xall = gather_all(
        query_weight, key_weight, value_weight, output_weight, inner_weight, outer_weight, vec, layer_input)
    small_all = jnp.transpose(vecs[:, :8, :24], (1, 0, 2)).reshape(8, width).astype(f32)
    query_b, value_b, output_b, gain_one, shift_one, outer_b, gain_two, shift_two = [small_all[n] for n in range(8)]
    inner_b = vecs[:, 8, :96].reshape(3072).astype(f32)

    tokens = layer_input.reshape(tokens_all, width)
    resid_in = tokens.astype(f32)
    flat = xall.reshape(seqs * keys, width)
    query = (plain_dot(tokens, wqkv[0]) + query_b).astype(bf).reshape(seqs, rows, width)
    every_key = plain_dot(flat, wqkv[1]).astype(bf).reshape(seqs, keys, width)
    every_value = (plain_dot(flat, wqkv[2]) + value_b).astype(bf).reshape(seqs, keys, width)

    ends = jnp.cumsum(doc_lengths, axis=1, dtype=jnp.int32)
    places = jnp.arange(keys, dtype=jnp.int32)
    segs = jnp.sum((places[None, :, None] >= ends[:, None, :-1]).astype(jnp.int32), axis=2)
    begin = lax.axis_index("ctx") * rows
    own_segs = lax.dynamic_slice_in_dim(segs, begin, rows, 1)
    starts = ends - doc_lengths
    low = jnp.max(jnp.where(starts <= begin, starts, 0), axis=1)
    high = jnp.min(jnp.where(ends > begin + rows - 1, ends, keys), axis=1)
    bounds = jnp.stack([low // KEYS, (high + KEYS - 1) // KEYS], axis=1).reshape(-1)
    qseg, kseg = own_segs[:, :, None], segs[:, None, :]

    mixed, total = attend(bounds, query, every_key, every_value, qseg, kseg)
    attn = mixed.reshape(tokens_all, width).astype(bf)
    branch = plain_dot(attn, wmid[0]) + output_b
    first, first_normed, first_inverse = layer_norm_parts(resid_in + branch, gain_one, shift_one)
    first_low = first.astype(bf)
    inner_w = jnp.concatenate([wmid[1], wmid[2], wmid[3], wmid[4]], axis=1)
    inner = plain_dot(first_low, inner_w) + inner_b
    act, act_pull = jax.vjp(gelu_exact, inner)
    act_low = act.astype(bf)
    outer = plain_dot(act_low, wlast) + outer_b
    final, second_normed, second_inverse = layer_norm_parts(first + outer, gain_two, shift_two)

    cotangent = output_cotangent.reshape(tokens_all, width).astype(f32)
    grad_two = norm_back(cotangent, second_normed, second_inverse, gain_two)
    grad_outer = grad_two.astype(bf)
    grad_inner = act_pull(right_dot(grad_outer, wlast))[0].astype(bf)
    grad_first = grad_two + right_dot(grad_inner, inner_w)
    grad_one = norm_back(grad_first, first_normed, first_inverse, gain_one)
    grad_branch = grad_one.astype(bf)
    grad_mixed = right_dot(grad_branch, wmid[0])

    grad_query, grad_keys, grad_values = attend_back(
        bounds, query, every_key, every_value, qseg, kseg, mixed, total, grad_mixed.reshape(seqs, rows, width))
    grad_query = grad_query.reshape(tokens_all, width)
    grad_keys = grad_keys.reshape(seqs * keys, width)
    grad_values = grad_values.reshape(seqs * keys, width)
    def over(value):
        return jnp.sum(value.astype(f32), axis=0)

    vg = jnp.concatenate([
        jnp.stack([over(grad_query), over(grad_values), over(grad_branch), over(grad_first * first_normed), over(grad_first),
                   over(grad_outer), over(cotangent * second_normed), over(cotangent)]),
        over(grad_inner).reshape(4, width), jnp.zeros((4, width), f32)])
    oq, oo, oin, oout, ox, ovec = reduce_all(
        act_low, grad_inner, first_low, grad_outer, attn, grad_branch, tokens, grad_query, flat, grad_keys, grad_values,
        wqkv, grad_one, vg)
    gq, gk, gv, go, gin, gout, gx = place(oq, oo, oin, oout, ox)
    small_out = [ovec[n, :24] for n in range(8)]
    return (final.astype(bf).reshape(seqs, rows, width), gx, gq, gk, gv, go, small_out[0], small_out[1], small_out[2],
            small_out[3], small_out[4], gin, ovec[8, :96], gout, small_out[5], small_out[6], small_out[7])


def solution(mesh):
    plan = local_fast if (mesh.shape["seq"], mesh.shape["ctx"]) == (4, 8) else local
    return jax.shard_map(
        plan,
        mesh=mesh,
        in_specs=(
            P("seq", "ctx", None),
            P("seq", None),
            P(("seq", "ctx"), None),
            P(("seq", "ctx"), None),
            P(("seq", "ctx"), None),
            P(("seq", "ctx"), None),
            P(("seq", "ctx")),
            P(("seq", "ctx")),
            P(("seq", "ctx")),
            P(("seq", "ctx")),
            P(("seq", "ctx")),
            P(("seq", "ctx"), None),
            P(("seq", "ctx")),
            P(("seq", "ctx"), None),
            P(("seq", "ctx")),
            P(("seq", "ctx")),
            P(("seq", "ctx")),
            P("seq", "ctx", None),
        ),
        out_specs=(
            P("seq", "ctx", None),
            P("seq", "ctx", None),
            P(("seq", "ctx"), None),
            P(("seq", "ctx"), None),
            P(("seq", "ctx"), None),
            P(("seq", "ctx"), None),
            P(("seq", "ctx")),
            P(("seq", "ctx")),
            P(("seq", "ctx")),
            P(("seq", "ctx")),
            P(("seq", "ctx")),
            P(("seq", "ctx"), None),
            P(("seq", "ctx")),
            P(("seq", "ctx"), None),
            P(("seq", "ctx")),
            P(("seq", "ctx")),
            P(("seq", "ctx")),
        ),
        check_vma=False,
    )
```
